32 devices in a mesh: seq: 8 (over z, x), ch: 4 (over y, core).
Axes of the slice: x: 2, y: 2, z: 4, core: 2. Of those that a mesh axis runs over, the one named last changes fastest.
Arguments:
- block_input: bfloat16 [131072, 2048], P('seq', 'ch'), may hold values from -6 to 6
- gate_pre: bfloat16 [131072, 2048], P('seq', 'ch'), may hold values from -8 to 8
- out_grad: bfloat16 [131072, 2048], P('seq', 'ch'), may hold values from -6 to 6
- block_weight: bfloat16 [256, 512, 512], P('seq', 'ch'), may hold values from -0.25 to 0.25
- offset_weight: bfloat16 [512, 256, 256], P(('seq', 'ch')), may hold values from -0.375 to 0.375
- out_weight: bfloat16 [2048, 2048], P(None, 'ch'), may hold values from -0.125 to 0.125
- reset_offset: int32 [256], replicated, may hold values from 0 to 512, as said below
Outputs:
- input_grad: bfloat16 [131072, 2048], P('seq', 'ch')
- gate_grad: bfloat16 [131072, 2048], P('seq', 'ch')
- block_grad: bfloat16 [256, 512, 512], P('seq', 'ch')
- offset_grad: bfloat16 [512, 256, 256], P(('seq', 'ch'))
- out_weight_grad: bfloat16 [2048, 2048], P('seq', 'ch')
The draws below stay inside these ranges and needn't reach their ends.
Inputs may be any that keep to these rules, and one draw needn't show every extreme that they name: reset_offset[0] is 0 and the last block starts no document; other blocks start a document at some place or none.
All inputs are finite; a program needn't handle non-finite values.
Results may differ from the reference program's by a relative error of at most 0.013.
Values may be sent and summed in bfloat16 or wider, within the bound.
No kernel may reach another device: no remote copies, remote signals or barrier semaphores. Data moves between devices by JAX's collectives and lax.ppermute only.
A program may use at most 512 MiB of HBM per device.

```python
import jax
import jax.numpy as jnp
from jax import lax

B1 = 512
NB = 256
D = 2048
L = 131072
N_CH = 4


def draw_reset_offset(key, part):
    key_start, key_place = jax.random.split(key)
    starts = jax.random.randint(key_start, (NB,), 0, 16) == 0
    places = jax.random.randint(key_place, (NB,), 1, B1)
    offsets = jnp.where(starts, places, B1)
    position = jnp.arange(NB)
    offsets = jnp.where(position == 0, 0, offsets)
    offsets = jnp.where(position == NB - 1, B1, offsets)
    return offsets.astype(jnp.int32)


def with_spikes(entries, rng, source, target, shards_of, factor):
    def block_of(dim):
        return (jnp.arange(entries.shape[dim]) // (entries.shape[dim] // shards_of)).reshape((-1,) + (1,) * (entries.ndim - 1 - dim))

    near = jax.random.permutation(rng, shards_of)[block_of(target)]
    other_side = (block_of(target) + shards_of // 2) % shards_of
    return jnp.where((block_of(source) == near) | (block_of(source) == other_side), factor * entries, entries)


def shard_levels(own_key, extent, cuts, least, top_value):
    def one(dim, blocks):
        draws = jax.random.uniform(jax.random.fold_in(jax.random.fold_in(own_key, 6), dim), (blocks,), jnp.float32, least / len(cuts), top_value / len(cuts))
        return jnp.repeat(jnp.exp(draws), extent[dim] // blocks).reshape((-1,) + (1,) * (len(extent) - dim - 1))

    level = one(*cuts[0])
    for cut in cuts[1:]:
        level = level * one(*cut)
    return level


def noise(key, shape, spread, most, shards=(), held_as=jnp.bfloat16):
    drawn = spread * jax.random.normal(key, shape, jnp.float32)
    if shards:
        drawn = drawn * shard_levels(key, shape, shards, -0.22, 0.18)
    return jnp.clip(drawn, -most, most).astype(held_as)


def noise_with(stream_key, shape, width, limit, cuts, heavy, held_as=jnp.bfloat16):
    entries = width * jax.random.normal(stream_key, shape, jnp.float32)
    if cuts:
        entries = entries * shard_levels(stream_key, shape, cuts, -0.22, 0.18)
    return jnp.clip(with_spikes(entries, jax.random.fold_in(stream_key, 3), *heavy), -limit, limit).astype(held_as)


def setup_inputs(seed: int = 0) -> dict:
    streams_of = jax.random.split(jax.random.key(seed), 8)
    return {
        "block_input": noise(streams_of[0], (L, D), 1.0, 6.0, ((0, 8), (1, 4))),
        "gate_pre": noise(streams_of[1], (L, D), 2.0, 8.0, ((0, 8), (1, 4))),
        "out_grad": noise_with(streams_of[2], (L, D), 1.0, 6.0, ((0, 8), (1, 4)), (0, 1, 8, 2.0)),
        "block_weight": noise(streams_of[3], (NB, B1, B1), B1 ** -0.5, 0.25, ((0, 8), (1, 4))),
        "offset_weight": noise(streams_of[4], (B1, NB, NB), NB ** -0.5, 0.375, ((0, 32),)),
        "out_weight": noise(streams_of[5], (D, D), D ** -0.5, 0.125, ((1, 4),)),
        "reset_offset": draw_reset_offset(jax.random.fold_in(streams_of[7], 71), 0),
    }


def document_ids(reset_offset):
    starts = (reset_offset < B1).astype(jnp.int32)
    earlier = jnp.cumsum(starts) - starts
    within = jnp.arange(B1, dtype=jnp.int32)
    return earlier[:, None] + (within[None, :] >= reset_offset[:, None]).astype(jnp.int32)


def block_sides(reset_offset):
    within = jnp.arange(B1, dtype=jnp.int32)
    return within[None, :] >= reset_offset[:, None]


def reference(block_input, gate_pre, out_grad, block_weight, offset_weight, out_weight, reset_offset):
    doc_table = document_ids(reset_offset)
    side_table = block_sides(reset_offset)
    inputs = block_input.reshape(NB, B1, D)

    def section_one(operands):
        weight, values, side_flags = operands
        masked = jnp.where(side_flags[:, None] == side_flags[None, :], weight, jnp.zeros_like(weight))
        return masked, jnp.dot(masked, values, preferred_element_type=jnp.float32).astype(jnp.bfloat16)

    masked_one, section_out = lax.map(section_one, (block_weight, inputs, side_table))
    section_cols = jnp.transpose(section_out, (1, 0, 2))
    doc_cols = doc_table.T

    def section_two(operands):
        weight, values, labels = operands
        masked = jnp.where(labels[:, None] == labels[None, :], weight, jnp.zeros_like(weight))
        return masked, jnp.dot(masked, values, preferred_element_type=jnp.float32).astype(jnp.bfloat16)

    masked_two, mixer_cols = lax.map(section_two, (offset_weight, section_cols, doc_cols))
    mixer_out = jnp.transpose(mixer_cols, (1, 0, 2))

    def gating(accumulated, operands):
        mixer_block, gate_block, grad_block = operands
        head_grad = jnp.dot(grad_block, out_weight, preferred_element_type=jnp.float32)
        sigmoid_gate = jax.nn.sigmoid(gate_block.astype(jnp.float32))
        mixer_float = mixer_block.astype(jnp.float32)
        gated_out = (mixer_float * sigmoid_gate).astype(jnp.bfloat16)
        accumulated = accumulated + jnp.dot(grad_block.T, gated_out, preferred_element_type=jnp.float32)
        mixer_grad = (head_grad * sigmoid_gate).astype(jnp.bfloat16)
        gate_grad = (head_grad * mixer_float * sigmoid_gate * (1.0 - sigmoid_gate)).astype(jnp.bfloat16)
        return accumulated, (mixer_grad, gate_grad)

    weight_sum, (mixer_grad, gate_grad) = lax.scan(
        gating, jnp.zeros((D, D), jnp.float32),
        (mixer_out, gate_pre.reshape(NB, B1, D), out_grad.reshape(NB, B1, D)))
    mixer_grad_cols = jnp.transpose(mixer_grad, (1, 0, 2))

    def section_two_back(operands):
        masked, values, gradients, labels = operands
        weight_grad = jnp.dot(gradients, values.T, preferred_element_type=jnp.float32)
        weight_grad = jnp.where(labels[:, None] == labels[None, :], weight_grad, jnp.zeros_like(weight_grad))
        returned = jnp.dot(masked.T, gradients, preferred_element_type=jnp.float32)
        return weight_grad.astype(jnp.bfloat16), returned.astype(jnp.bfloat16)

    offset_grad, section_grad_cols = lax.map(section_two_back, (masked_two, section_cols, mixer_grad_cols, doc_cols))
    section_grad = jnp.transpose(section_grad_cols, (1, 0, 2))
    shard_width = D // N_CH

    def section_one_back(operands):
        masked, values, gradients, side_flags = operands
        summed = jnp.zeros((B1, B1), jnp.float32)
        for shard_index in range(N_CH):
            first_col = shard_index * shard_width
            partial_value = jnp.dot(gradients[:, first_col:first_col + shard_width],
                              values[:, first_col:first_col + shard_width].T,
                              preferred_element_type=jnp.float32)
            rounded = lax.optimization_barrier(partial_value.astype(jnp.bfloat16))
            summed = summed + rounded.astype(jnp.float32)
        summed = jnp.where(side_flags[:, None] == side_flags[None, :], summed, jnp.zeros_like(summed))
        returned = jnp.dot(masked.T, gradients, preferred_element_type=jnp.float32)
        return summed.astype(jnp.bfloat16), returned.astype(jnp.bfloat16)

    block_grad, input_grad = lax.map(section_one_back, (masked_one, inputs, section_grad, side_table))
    return (input_grad.reshape(NB * B1, D), gate_grad.reshape(NB * B1, D), block_grad, offset_grad,
            weight_sum.astype(jnp.bfloat16))
```

```python
import jax
import jax.numpy as jnp
from jax import lax
from jax.sharding import PartitionSpec as P


IN_ONE = (2, 4, 10)
IN_TWO = (8, 8)
OUT_ONE = (16,)
OUT_TWO = (9, 5, 2)


def side_flags_of(reset_offset, block_span):
    within = jnp.arange(block_span, dtype=jnp.int32)
    return within[None, :] >= reset_offset[:, None]


def document_ids(reset_offset, block_span):
    starts = (reset_offset < block_span).astype(jnp.int32)
    earlier = jnp.cumsum(starts) - starts
    return earlier[:, None] + side_flags_of(reset_offset, block_span).astype(jnp.int32)


def spans_of(shares, block_count):
    cuts = [0]
    for share in shares:
        cuts.append(cuts[-1] + share)
    cuts = [cut * block_count // 16 for cut in cuts]
    return list(zip(cuts, cuts[1:]))


def scatter_sum(part, axis_name, dim):
    count = lax.axis_size(axis_name)
    index = lax.axis_index(axis_name)
    shape = part.shape
    part = part.reshape(*shape[:dim], count, shape[dim] // count, *shape[dim + 1 :])
    for n in range((count - 1).bit_length()):
        left = part.shape[dim] // 2
        part = part.reshape(*part.shape[:dim], left, 2, *part.shape[dim + 1 :])
        bit = (index >> n) & 1
        kept = lax.dynamic_index_in_dim(part, bit, dim + 1, keepdims=False)
        sent = lax.dynamic_index_in_dim(part, 1 - bit, dim + 1, keepdims=False)
        came = lax.ppermute(sent, axis_name, [(i, i ^ (1 << n)) for i in range(count)])
        part = (kept.astype(jnp.float32) + came.astype(jnp.float32)).astype(part.dtype)
    return part.reshape(*shape[:dim], shape[dim] // count, *shape[dim + 1 :])


def to_offsets(blocked, seq_count):
    count, block_span, channels = blocked.shape
    places = block_span // seq_count
    split = blocked.reshape(count, seq_count, places, channels).transpose(1, 0, 2, 3)
    return lax.all_to_all(split, "seq", split_axis=0, concat_axis=0, tiled=True)


def to_blocks(spread, seq_count):
    arrived = lax.all_to_all(spread, "seq", split_axis=0, concat_axis=0, tiled=True)
    count, places, channels = arrived.shape[1:]
    return arrived.transpose(1, 0, 2, 3).reshape(count, seq_count * places, channels)


def on_device(
    block_input, gate_pre, out_grad, block_weight, offset_weight, out_weight, reset_offset
):
    seq_count = lax.axis_size("seq")
    token_count, channels = block_input.shape
    block_span = block_weight.shape[2]
    block_count = token_count // block_span
    places = block_span // seq_count
    seq_index = lax.axis_index("seq")
    side_table = side_flags_of(reset_offset, block_span)
    doc_table = document_ids(reset_offset, block_span)
    total_blocks = doc_table.shape[0]
    local_sides = lax.dynamic_slice_in_dim(side_table, seq_index * block_count, block_count, 0)
    inputs = block_input.reshape(block_count, block_span, channels)
    gates = gate_pre.reshape(block_count, block_span, channels)
    grads = out_grad.reshape(block_count, block_span, channels)

    def mask_one(lo, hi):
        sides = local_sides[lo:hi]
        return sides[:, :, None] == sides[:, None, :]

    weights, section_parts = [], []
    for lo, hi in spans_of(IN_ONE, block_count):
        gathered = lax.all_gather(block_weight[lo:hi], "ch", axis=1, tiled=True)
        masked = jnp.where(mask_one(lo, hi), gathered, jnp.zeros_like(gathered))
        weights.append(gathered)
        section = jnp.einsum(
            "ikj,ijd->ikd", masked, inputs[lo:hi], preferred_element_type=jnp.float32
        ).astype(jnp.bfloat16)
        section_parts.append(to_offsets(section, seq_count))
    full_weight = jnp.concatenate(weights, axis=0)
    section_spread = jnp.concatenate(section_parts, axis=1)

    full_grads, mixer_grads, grad_parts = [], [], []
    for lo, hi in spans_of(IN_TWO, block_count):
        gathered = lax.all_gather(grads[lo:hi], "ch", axis=2, tiled=True)
        full_grads.append(gathered)
        head_grad = jnp.dot(
            gathered.reshape(-1, out_weight.shape[0]),
            out_weight,
            preferred_element_type=jnp.float32,
        ).reshape(hi - lo, block_span, channels)
        sigmoid_gate = jax.nn.sigmoid(gates[lo:hi].astype(jnp.float32))
        mixer_grad = (head_grad * sigmoid_gate).astype(jnp.bfloat16)
        mixer_grads.append(mixer_grad)
        grad_parts.append(to_offsets(mixer_grad, seq_count))
    grad_spread = jnp.concatenate(grad_parts, axis=1)

    own_offsets = lax.all_gather(offset_weight, "ch", axis=0, tiled=True)
    labels = lax.dynamic_slice_in_dim(doc_table, seq_index * places, places, 1).T
    mask_two = labels[:, :, None] == labels[:, None, :]
    masked_two = jnp.where(mask_two, own_offsets, jnp.zeros_like(own_offsets))
    section_spread = section_spread.reshape(total_blocks, places, channels)
    grad_spread = grad_spread.reshape(total_blocks, places, channels)
    mixer_spread = jnp.einsum(
        "kmi,ikd->mkd", masked_two, section_spread, preferred_element_type=jnp.float32
    ).astype(jnp.bfloat16)
    mixer_spread = mixer_spread.reshape(seq_count, block_count, places, channels)
    mixer_parts = []
    for lo, hi in spans_of(OUT_ONE, block_count):
        mixer_parts.append(to_blocks(mixer_spread[:, lo:hi], seq_count))
    mixer_out = jnp.concatenate(mixer_parts)
    section_grad_spread = jnp.einsum(
        "kmi,mkd->ikd", masked_two, grad_spread, preferred_element_type=jnp.float32
    ).astype(jnp.bfloat16)
    section_grad_spread = section_grad_spread.reshape(seq_count, block_count, places, channels)
    offset_grad = jnp.einsum(
        "mkd,ikd->kmi", grad_spread, section_spread, preferred_element_type=jnp.float32
    )
    offset_grad = jnp.where(mask_two, offset_grad, jnp.zeros_like(offset_grad)).astype(jnp.bfloat16)
    offset_grad = lax.psum_scatter(offset_grad, "ch", scatter_dimension=0, tiled=True)

    full_grad = jnp.concatenate(full_grads, axis=0).reshape(token_count, -1)
    mixer_grad = jnp.concatenate(mixer_grads, axis=0)
    later_gates, mixer_out = lax.optimization_barrier((gates, mixer_out))
    sigmoid_gate = jax.nn.sigmoid(later_gates.astype(jnp.float32))
    mixer_float = mixer_out.astype(jnp.float32)
    gated_out = (mixer_float * sigmoid_gate).astype(jnp.bfloat16)
    gate_grad = (mixer_grad.astype(jnp.float32) * mixer_float * (1.0 - sigmoid_gate)).astype(
        jnp.bfloat16
    )
    weight_part = jnp.einsum(
        "te,tc->ec",
        full_grad,
        gated_out.reshape(token_count, channels),
        preferred_element_type=jnp.float32,
    ).astype(jnp.bfloat16)
    weight_share = scatter_sum(weight_part, "seq", 0)

    block_grad = jnp.zeros(block_weight.shape, jnp.bfloat16)
    input_grad = jnp.zeros(inputs.shape, jnp.bfloat16)
    for n, (lo, hi) in enumerate(spans_of(OUT_TWO, block_count)):
        section_grad = to_blocks(section_grad_spread[:, lo:hi], seq_count)
        mask = mask_one(lo, hi)
        partial_grad = jnp.einsum(
            "ikd,ijd->ikj", section_grad, inputs[lo:hi], preferred_element_type=jnp.float32
        )
        partial_grad = jnp.where(mask, partial_grad, jnp.zeros_like(partial_grad))
        partial_grad = partial_grad.astype(jnp.bfloat16)
        if n == len(OUT_TWO) - 1:
            reduced = scatter_sum(partial_grad, "ch", 1)
        else:
            reduced = lax.psum_scatter(partial_grad, "ch", scatter_dimension=1, tiled=True)
        block_grad = lax.dynamic_update_slice(block_grad, reduced, (lo, 0, 0))
        weight = full_weight[lo:hi]
        masked = jnp.where(mask, weight, jnp.zeros_like(weight))
        returned = jnp.einsum(
            "ikj,ikd->ijd", masked, section_grad, preferred_element_type=jnp.float32
        ).astype(jnp.bfloat16)
        input_grad = lax.dynamic_update_slice(input_grad, returned, (lo, 0, 0))
    return (
        input_grad.reshape(token_count, channels),
        gate_grad.reshape(token_count, channels),
        block_grad,
        offset_grad,
        weight_share,
    )


def solution(mesh):
    in_specs = (
        P("seq", "ch"),
        P("seq", "ch"),
        P("seq", "ch"),
        P("seq", "ch", None),
        P(("seq", "ch"), None, None),
        P(None, "ch"),
        P(),
    )
    out_specs = (
        P("seq", "ch"),
        P("seq", "ch"),
        P("seq", "ch", None),
        P(("seq", "ch"), None, None),
        P("seq", "ch"),
    )
    return jax.shard_map(
        on_device, mesh=mesh, in_specs=in_specs, out_specs=out_specs, check_vma=False
    )
```

```python
import jax
import jax.numpy as jnp
from jax import lax
from jax.sharding import PartitionSpec as P


IN_ONE = (2, 4, 10)
IN_TWO = (8, 8)
OUT_ONE = (16,)
OUT_TWO = (9, 5, 2)


def side_flags_of(reset_offset, block_span):
    within = jnp.arange(block_span, dtype=jnp.int32)
    return within[None, :] >= reset_offset[:, None]


def document_ids(reset_offset, block_span):
    starts = (reset_offset < block_span).astype(jnp.int32)
    earlier = jnp.cumsum(starts) - starts
    return earlier[:, None] + side_flags_of(reset_offset, block_span).astype(jnp.int32)


def spans_of(shares, block_count):
    cuts = [0]
    for share in shares:
        cuts.append(cuts[-1] + share)
    cuts = [cut * block_count // 16 for cut in cuts]
    return list(zip(cuts, cuts[1:]))


def scatter_sum(part, axis_name, dim):
    count = lax.axis_size(axis_name)
    index = lax.axis_index(axis_name)
    shape = part.shape
    part = part.reshape(*shape[:dim], count, shape[dim] // count, *shape[dim + 1 :])
    for n in range((count - 1).bit_length()):
        left = part.shape[dim] // 2
        part = part.reshape(*part.shape[:dim], left, 2, *part.shape[dim + 1 :])
        bit = (index >> n) & 1
        kept = lax.dynamic_index_in_dim(part, bit, dim + 1, keepdims=False)
        sent = lax.dynamic_index_in_dim(part, 1 - bit, dim + 1, keepdims=False)
        came = lax.ppermute(sent, axis_name, [(i, i ^ (1 << n)) for i in range(count)])
        part = (kept.astype(jnp.float32) + came.astype(jnp.float32)).astype(part.dtype)
    return part.reshape(*shape[:dim], shape[dim] // count, *shape[dim + 1 :])


def swapped(spread, seq_count):
    index = lax.axis_index("seq")
    came = {}
    for n in reversed(range(1, seq_count)):
        piece = lax.dynamic_index_in_dim(spread, index ^ n, 0)
        came[n] = lax.ppermute(piece, "seq", [(i, i ^ n) for i in range(seq_count)])
    for n in range(1, seq_count):
        spread = lax.dynamic_update_index_in_dim(spread, came[n], index ^ n, 0)
    return spread


def traded(spread, seq_count, by_permutes):
    if by_permutes:
        return swapped(spread, seq_count)
    return lax.all_to_all(spread, "seq", split_axis=0, concat_axis=0, tiled=True)


def to_offsets(blocked, seq_count, by_permutes=False):
    count, block_span, channels = blocked.shape
    places = block_span // seq_count
    split = blocked.reshape(count, seq_count, places, channels).transpose(1, 0, 2, 3)
    return traded(split, seq_count, by_permutes)


def to_blocks(spread, seq_count, by_permutes=False):
    arrived = traded(spread, seq_count, by_permutes)
    count, places, channels = arrived.shape[1:]
    return arrived.transpose(1, 0, 2, 3).reshape(count, seq_count * places, channels)


def on_device(
    block_input, gate_pre, out_grad, block_weight, offset_weight, out_weight, reset_offset
):
    seq_count = lax.axis_size("seq")
    token_count, channels = block_input.shape
    block_span = block_weight.shape[2]
    block_count = token_count // block_span
    places = block_span // seq_count
    seq_index = lax.axis_index("seq")
    side_table = side_flags_of(reset_offset, block_span)
    doc_table = document_ids(reset_offset, block_span)
    total_blocks = doc_table.shape[0]
    local_sides = lax.dynamic_slice_in_dim(side_table, seq_index * block_count, block_count, 0)
    inputs = block_input.reshape(block_count, block_span, channels)
    gates = gate_pre.reshape(block_count, block_span, channels)
    grads = out_grad.reshape(block_count, block_span, channels)

    def mask_one(lo, hi):
        sides = local_sides[lo:hi]
        return sides[:, :, None] == sides[:, None, :]

    weights, section_parts = [], []
    for n, (lo, hi) in enumerate(spans_of(IN_ONE, block_count)):
        gathered = lax.all_gather(block_weight[lo:hi], "ch", axis=1, tiled=True)
        masked = jnp.where(mask_one(lo, hi), gathered, jnp.zeros_like(gathered))
        weights.append(gathered)
        section = jnp.einsum(
            "ikj,ijd->ikd", masked, inputs[lo:hi], preferred_element_type=jnp.float32
        ).astype(jnp.bfloat16)
        section_parts.append(to_offsets(section, seq_count, n > 0))
    full_weight = jnp.concatenate(weights, axis=0)
    section_spread = jnp.concatenate(section_parts, axis=1)

    full_grads, mixer_grads, grad_parts = [], [], []
    for n, (lo, hi) in enumerate(spans_of(IN_TWO, block_count)):
        gathered = lax.all_gather(grads[lo:hi], "ch", axis=2, tiled=True)
        full_grads.append(gathered)
        head_grad = jnp.dot(
            gathered.reshape(-1, out_weight.shape[0]),
            out_weight,
            preferred_element_type=jnp.float32,
        ).reshape(hi - lo, block_span, channels)
        sigmoid_gate = jax.nn.sigmoid(gates[lo:hi].astype(jnp.float32))
        mixer_grad = (head_grad * sigmoid_gate).astype(jnp.bfloat16)
        mixer_grads.append(mixer_grad)
        grad_parts.append(to_offsets(mixer_grad, seq_count, n > 0))
    grad_spread = jnp.concatenate(grad_parts, axis=1)

    own_offsets = lax.all_gather(offset_weight, "ch", axis=0, tiled=True)
    labels = lax.dynamic_slice_in_dim(doc_table, seq_index * places, places, 1).T
    mask_two = labels[:, :, None] == labels[:, None, :]
    masked_two = jnp.where(mask_two, own_offsets, jnp.zeros_like(own_offsets))
    section_spread = section_spread.reshape(total_blocks, places, channels)
    grad_spread = grad_spread.reshape(total_blocks, places, channels)
    mixer_spread = jnp.einsum(
        "kmi,ikd->mkd", masked_two, section_spread, preferred_element_type=jnp.float32
    ).astype(jnp.bfloat16)
    mixer_spread = mixer_spread.reshape(seq_count, block_count, places, channels)
    mixer_parts = []
    for lo, hi in spans_of(OUT_ONE, block_count):
        mixer_parts.append(to_blocks(mixer_spread[:, lo:hi], seq_count, True))
    mixer_out = jnp.concatenate(mixer_parts)
    section_grad_spread = jnp.einsum(
        "kmi,mkd->ikd", masked_two, grad_spread, preferred_element_type=jnp.float32
    ).astype(jnp.bfloat16)
    section_grad_spread = section_grad_spread.reshape(seq_count, block_count, places, channels)
    offset_grad = jnp.einsum(
        "mkd,ikd->kmi", grad_spread, section_spread, preferred_element_type=jnp.float32
    )
    offset_grad = jnp.where(mask_two, offset_grad, jnp.zeros_like(offset_grad)).astype(jnp.bfloat16)
    offset_grad = lax.psum_scatter(offset_grad, "ch", scatter_dimension=0, tiled=True)

    full_grad = jnp.concatenate(full_grads, axis=0).reshape(token_count, -1)
    mixer_grad = jnp.concatenate(mixer_grads, axis=0)
    later_gates, mixer_out = lax.optimization_barrier((gates, mixer_out))
    sigmoid_gate = jax.nn.sigmoid(later_gates.astype(jnp.float32))
    mixer_float = mixer_out.astype(jnp.float32)
    gated_out = (mixer_float * sigmoid_gate).astype(jnp.bfloat16)
    gate_grad = (mixer_grad.astype(jnp.float32) * mixer_float * (1.0 - sigmoid_gate)).astype(
        jnp.bfloat16
    )
    weight_part = jnp.einsum(
        "te,tc->ec",
        full_grad,
        gated_out.reshape(token_count, channels),
        preferred_element_type=jnp.float32,
    ).astype(jnp.bfloat16)
    weight_share = scatter_sum(weight_part, "seq", 0)

    block_grad = jnp.zeros(block_weight.shape, jnp.bfloat16)
    input_grad = jnp.zeros(inputs.shape, jnp.bfloat16)
    for n, (lo, hi) in enumerate(spans_of(OUT_TWO, block_count)):
        section_grad = to_blocks(section_grad_spread[:, lo:hi], seq_count)
        mask = mask_one(lo, hi)
        partial_grad = jnp.einsum(
            "ikd,ijd->ikj", section_grad, inputs[lo:hi], preferred_element_type=jnp.float32
        )
        partial_grad = jnp.where(mask, partial_grad, jnp.zeros_like(partial_grad))
        partial_grad = partial_grad.astype(jnp.bfloat16)
        if n == len(OUT_TWO) - 1:
            reduced = scatter_sum(partial_grad, "ch", 1)
        else:
            reduced = lax.psum_scatter(partial_grad, "ch", scatter_dimension=1, tiled=True)
        block_grad = lax.dynamic_update_slice(block_grad, reduced, (lo, 0, 0))
        weight = full_weight[lo:hi]
        masked = jnp.where(mask, weight, jnp.zeros_like(weight))
        returned = jnp.einsum(
            "ikj,ikd->ijd", masked, section_grad, preferred_element_type=jnp.float32
        ).astype(jnp.bfloat16)
        input_grad = lax.dynamic_update_slice(input_grad, returned, (lo, 0, 0))
    return (
        input_grad.reshape(token_count, channels),
        gate_grad.reshape(token_count, channels),
        block_grad,
        offset_grad,
        weight_share,
    )


def solution(mesh):
    in_specs = (
        P("seq", "ch"),
        P("seq", "ch"),
        P("seq", "ch"),
        P("seq", "ch", None),
        P(("seq", "ch"), None, None),
        P(None, "ch"),
        P(),
    )
    out_specs = (
        P("seq", "ch"),
        P("seq", "ch"),
        P("seq", "ch", None),
        P(("seq", "ch"), None, None),
        P("seq", "ch"),
    )
    return jax.shard_map(
        on_device, mesh=mesh, in_specs=in_specs, out_specs=out_specs, check_vma=False
    )
```

```python
import jax
import jax.numpy as jnp
from jax import lax
from jax.sharding import PartitionSpec as P


IN_ONE = (1, 2, 4, 9)
IN_TWO = (8, 8)
OUT_ONE = (16,)
OUT_TWO = (9, 4, 2, 1)


def side_flags_of(reset_offset, block_span):
    within = jnp.arange(block_span, dtype=jnp.int32)
    return within[None, :] >= reset_offset[:, None]


def document_ids(reset_offset, block_span):
    starts = (reset_offset < block_span).astype(jnp.int32)
    earlier = jnp.cumsum(starts) - starts
    return earlier[:, None] + side_flags_of(reset_offset, block_span).astype(jnp.int32)


def spans_of(shares, block_count):
    cuts = [0]
    for share in shares:
        cuts.append(cuts[-1] + share)
    cuts = [cut * block_count // 16 for cut in cuts]
    return [span for span in zip(cuts, cuts[1:]) if span[0] < span[1]]


def scatter_sum(part, axis_name, dim):
    count = lax.axis_size(axis_name)
    index = lax.axis_index(axis_name)
    shape = part.shape
    part = part.reshape(*shape[:dim], count, shape[dim] // count, *shape[dim + 1 :])
    for n in range((count - 1).bit_length()):
        left = part.shape[dim] // 2
        part = part.reshape(*part.shape[:dim], left, 2, *part.shape[dim + 1 :])
        bit = (index >> n) & 1
        kept = lax.dynamic_index_in_dim(part, bit, dim + 1, keepdims=False)
        sent = lax.dynamic_index_in_dim(part, 1 - bit, dim + 1, keepdims=False)
        came = lax.ppermute(sent, axis_name, [(i, i ^ (1 << n)) for i in range(count)])
        part = (kept.astype(jnp.float32) + came.astype(jnp.float32)).astype(part.dtype)
    return part.reshape(*shape[:dim], shape[dim] // count, *shape[dim + 1 :])


def swapped(spread, seq_count):
    index = lax.axis_index("seq")
    came = {}
    for n in reversed(range(1, seq_count)):
        piece = lax.dynamic_index_in_dim(spread, index ^ n, 0)
        came[n] = lax.ppermute(piece, "seq", [(i, i ^ n) for i in range(seq_count)])
    for n in range(1, seq_count):
        spread = lax.dynamic_update_index_in_dim(spread, came[n], index ^ n, 0)
    return spread


def traded(spread, seq_count, by_permutes):
    if by_permutes:
        return swapped(spread, seq_count)
    return lax.all_to_all(spread, "seq", split_axis=0, concat_axis=0, tiled=True)


def to_offsets(blocked, seq_count, by_permutes=False):
    count, block_span, channels = blocked.shape
    places = block_span // seq_count
    split = blocked.reshape(count, seq_count, places, channels).transpose(1, 0, 2, 3)
    return traded(split, seq_count, by_permutes)


def to_blocks(spread, seq_count, by_permutes=False):
    arrived = traded(spread, seq_count, by_permutes)
    count, places, channels = arrived.shape[1:]
    return arrived.transpose(1, 0, 2, 3).reshape(count, seq_count * places, channels)


def on_device(
    block_input, gate_pre, out_grad, block_weight, offset_weight, out_weight, reset_offset
):
    seq_count = lax.axis_size("seq")
    token_count, channels = block_input.shape
    block_span = block_weight.shape[2]
    block_count = token_count // block_span
    places = block_span // seq_count
    seq_index = lax.axis_index("seq")
    side_table = side_flags_of(reset_offset, block_span)
    doc_table = document_ids(reset_offset, block_span)
    total_blocks = doc_table.shape[0]
    local_sides = lax.dynamic_slice_in_dim(side_table, seq_index * block_count, block_count, 0)
    inputs = block_input.reshape(block_count, block_span, channels)
    gates = gate_pre.reshape(block_count, block_span, channels)
    grads = out_grad.reshape(block_count, block_span, channels)

    def mask_one(lo, hi):
        sides = local_sides[lo:hi]
        return sides[:, :, None] == sides[:, None, :]

    weights, section_parts = [], []
    for n, (lo, hi) in enumerate(spans_of(IN_ONE, block_count)):
        gathered = lax.all_gather(block_weight[lo:hi], "ch", axis=1, tiled=True)
        masked = jnp.where(mask_one(lo, hi), gathered, jnp.zeros_like(gathered))
        weights.append(gathered)
        section = jnp.einsum(
            "ikj,ijd->ikd", masked, inputs[lo:hi], preferred_element_type=jnp.float32
        ).astype(jnp.bfloat16)
        section_parts.append(to_offsets(section, seq_count, n > 0))
    full_weight = jnp.concatenate(weights, axis=0)
    section_spread = jnp.concatenate(section_parts, axis=1)

    full_grads, mixer_grads, grad_parts = [], [], []
    for n, (lo, hi) in enumerate(spans_of(IN_TWO, block_count)):
        gathered = lax.all_gather(grads[lo:hi], "ch", axis=2, tiled=True)
        full_grads.append(gathered)
        head_grad = jnp.dot(
            gathered.reshape(-1, out_weight.shape[0]),
            out_weight,
            preferred_element_type=jnp.float32,
        ).reshape(hi - lo, block_span, channels)
        sigmoid_gate = jax.nn.sigmoid(gates[lo:hi].astype(jnp.float32))
        mixer_grad = (head_grad * sigmoid_gate).astype(jnp.bfloat16)
        mixer_grads.append(mixer_grad)
        grad_parts.append(to_offsets(mixer_grad, seq_count, n > 0))
    grad_spread = jnp.concatenate(grad_parts, axis=1)

    own_offsets = lax.all_gather(offset_weight, "ch", axis=0, tiled=True)
    labels = lax.dynamic_slice_in_dim(doc_table, seq_index * places, places, 1).T
    mask_two = labels[:, :, None] == labels[:, None, :]
    masked_two = jnp.where(mask_two, own_offsets, jnp.zeros_like(own_offsets))
    section_spread = section_spread.reshape(total_blocks, places, channels)
    grad_spread = grad_spread.reshape(total_blocks, places, channels)
    mixer_spread = jnp.einsum(
        "kmi,ikd->mkd", masked_two, section_spread, preferred_element_type=jnp.float32
    ).astype(jnp.bfloat16)
    mixer_spread = mixer_spread.reshape(seq_count, block_count, places, channels)
    mixer_parts = []
    for lo, hi in spans_of(OUT_ONE, block_count):
        mixer_parts.append(to_blocks(mixer_spread[:, lo:hi], seq_count, True))
    mixer_out = jnp.concatenate(mixer_parts)
    section_grad_spread = jnp.einsum(
        "kmi,mkd->ikd", masked_two, grad_spread, preferred_element_type=jnp.float32
    ).astype(jnp.bfloat16)
    section_grad_spread = section_grad_spread.reshape(seq_count, block_count, places, channels)
    offset_grad = jnp.einsum(
        "mkd,ikd->kmi", grad_spread, section_spread, preferred_element_type=jnp.float32
    )
    offset_grad = jnp.where(mask_two, offset_grad, jnp.zeros_like(offset_grad)).astype(jnp.bfloat16)
    offset_grad = lax.psum_scatter(offset_grad, "ch", scatter_dimension=0, tiled=True)

    full_grad = jnp.concatenate(full_grads, axis=0).reshape(token_count, -1)
    mixer_grad = jnp.concatenate(mixer_grads, axis=0)
    later_gates, mixer_out = lax.optimization_barrier((gates, mixer_out))
    sigmoid_gate = jax.nn.sigmoid(later_gates.astype(jnp.float32))
    mixer_float = mixer_out.astype(jnp.float32)
    gated_out = (mixer_float * sigmoid_gate).astype(jnp.bfloat16)
    gate_grad = (mixer_grad.astype(jnp.float32) * mixer_float * (1.0 - sigmoid_gate)).astype(
        jnp.bfloat16
    )
    weight_part = jnp.einsum(
        "te,tc->ec",
        full_grad,
        gated_out.reshape(token_count, channels),
        preferred_element_type=jnp.float32,
    ).astype(jnp.bfloat16)
    weight_share = scatter_sum(weight_part, "seq", 0)

    block_grad = jnp.zeros(block_weight.shape, jnp.bfloat16)
    input_grad = jnp.zeros(inputs.shape, jnp.bfloat16)
    for n, (lo, hi) in enumerate(spans_of(OUT_TWO, block_count)):
        section_grad = to_blocks(section_grad_spread[:, lo:hi], seq_count)
        mask = mask_one(lo, hi)
        partial_grad = jnp.einsum(
            "ikd,ijd->ikj", section_grad, inputs[lo:hi], preferred_element_type=jnp.float32
        )
        partial_grad = jnp.where(mask, partial_grad, jnp.zeros_like(partial_grad))
        partial_grad = partial_grad.astype(jnp.bfloat16)
        if n > 1:
            reduced = scatter_sum(partial_grad, "ch", 1)
        else:
            reduced = lax.psum_scatter(partial_grad, "ch", scatter_dimension=1, tiled=True)
        block_grad = lax.dynamic_update_slice(block_grad, reduced, (lo, 0, 0))
        weight = full_weight[lo:hi]
        masked = jnp.where(mask, weight, jnp.zeros_like(weight))
        returned = jnp.einsum(
            "ikj,ikd->ijd", masked, section_grad, preferred_element_type=jnp.float32
        ).astype(jnp.bfloat16)
        input_grad = lax.dynamic_update_slice(input_grad, returned, (lo, 0, 0))
    return (
        input_grad.reshape(token_count, channels),
        gate_grad.reshape(token_count, channels),
        block_grad,
        offset_grad,
        weight_share,
    )


def solution(mesh):
    in_specs = (
        P("seq", "ch"),
        P("seq", "ch"),
        P("seq", "ch"),
        P("seq", "ch", None),
        P(("seq", "ch"), None, None),
        P(None, "ch"),
        P(),
    )
    out_specs = (
        P("seq", "ch"),
        P("seq", "ch"),
        P("seq", "ch", None),
        P(("seq", "ch"), None, None),
        P("seq", "ch"),
    )
    return jax.shard_map(
        on_device, mesh=mesh, in_specs=in_specs, out_specs=out_specs, check_vma=False
    )
```
